512 devices in a mesh: freq: 128 (over z, y, core), panel: 4 (over x).
Axes of the slice: x: 4, y: 8, z: 8, core: 2. Of those that a mesh axis runs over, the one named last changes fastest.
Arguments:
- wave: bfloat16 [2, 128, 1600, 1600], P(None, 'freq', 'panel'), may hold values from -0.15625 to 0.15625
- observed: float32 [4, 6400, 512], P('panel', 'freq'), may hold values from -25 to 25
Outputs:
- solution: float32 [25600, 512], P('freq')
The draws below stay inside these ranges and needn't reach their ends.
All inputs are finite; a program needn't handle non-finite values.
Results may differ from the reference program's by a relative error of at most 0.0085.
Values may be sent and summed in bfloat16 or wider, within the bound.
A program may use at most 64 MiB of HBM per device.

```python
import math
import jax
import jax.numpy as jnp
from jax import lax

S = 1600
R = 1600
VS = 16
NT = 512
ITERS = 3
F = 128
RP = 400
N_PANEL = 4


def draw_observed(key, part):
    total_rows = R * VS
    first, second = jax.random.split(key, 2)
    ramp = jnp.arange(total_rows, dtype=jnp.float32) / (total_rows - 1)
    row_scale = 10.0 ** ramp
    column_scale = 10.0 ** jax.random.uniform(second, (NT,), jnp.float32)
    values = 0.05 * jnp.clip(jax.random.normal(first, (total_rows, NT), jnp.float32), -5.0, 5.0)
    values = row_scale[:, None] * column_scale[None, :] * values
    return values.reshape(R // RP, VS * RP, NT)


def level_of(key, dims, cuts, least, high):
    loudness, own = 1.0, jax.random.fold_in(key, 6)
    for dim, shards_of in cuts:
        draws = jnp.exp(jax.random.uniform(jax.random.fold_in(own, dim), (shards_of,), jnp.float32, least / len(cuts), high / len(cuts)))
        loudness = loudness * jnp.repeat(draws, dims[dim] // shards_of).reshape([-1 if axis == dim else 1 for axis in range(len(dims))])
    return loudness


def centred(key, dims, scale, reach, cuts=(), held_as=jnp.bfloat16):
    values = jax.random.normal(key, dims, jnp.float32) * scale
    if len(cuts) > 0:
        values = level_of(key, dims, cuts, -0.22, 0.18) * values
    return jnp.clip(values, min=-reach, max=reach).astype(held_as)


def setup_inputs(seed: int = 0) -> dict:
    keys = jax.random.split(jax.random.key(seed), 3)
    wave = centred(keys[0], (2, F, R, S), S ** -0.5, 0.15625, ((1, 128), (2, 4)))
    observed = draw_observed(jax.random.fold_in(keys[2], 71), 0)
    return dict(wave=wave, observed=observed)


precise = lax.Precision.HIGHEST
epsilon = 1e-06

def transform_tables():
    freq_index = jnp.arange(F, dtype=jnp.int32)[:, None] + 1
    time_index = jnp.arange(NT, dtype=jnp.int32)[None, :]
    phases = (freq_index * time_index % NT).astype(jnp.float32) * (2.0 * math.pi / NT)
    factor = math.sqrt(2.0 / NT)
    return jnp.stack([factor * jnp.cos(phases), -factor * jnp.sin(phases)])

def to_spectrum(rows, table):
    return jnp.einsum('cft,rt->cfr', table, rows, precision=precise)

def from_spectrum(spectrum, table):
    return jnp.einsum('cft,cfr->rt', table, spectrum, precision=precise)

def forward_op(model, wave, table):
    spectrum = to_spectrum(model, table).astype(jnp.bfloat16).reshape(2, F, VS, S)

    def per_frequency(index):
        wave_here = lax.dynamic_index_in_dim(wave, index, 1, keepdims=False)
        spec_here = lax.dynamic_index_in_dim(spectrum, index, 1, keepdims=False)
        real_out = jnp.dot(spec_here[0], wave_here[0].T, preferred_element_type=jnp.float32) - jnp.dot(spec_here[1], wave_here[1].T, preferred_element_type=jnp.float32)
        imag_out = jnp.dot(spec_here[0], wave_here[1].T, preferred_element_type=jnp.float32) + jnp.dot(spec_here[1], wave_here[0].T, preferred_element_type=jnp.float32)
        return jnp.stack([real_out, imag_out]).astype(jnp.bfloat16)
    result = lax.map(per_frequency, jnp.arange(F, dtype=jnp.int32))
    result = result.reshape(F, 2, VS, N_PANEL, R // N_PANEL).transpose(1, 0, 3, 2, 4).reshape(2, F, R * VS)
    return from_spectrum(result.astype(jnp.float32), table).reshape(N_PANEL, VS * (R // N_PANEL), NT)

def adjoint_op(data, wave, table):
    lines = to_spectrum(data.reshape(R * VS, NT), table).astype(jnp.bfloat16)
    spectrum = lines.reshape(2, F, N_PANEL, VS, R // N_PANEL).transpose(0, 1, 3, 2, 4).reshape(2, F, VS, R)

    def per_frequency(index):
        wave_here = lax.dynamic_index_in_dim(wave, index, 1, keepdims=False)
        spec_here = lax.dynamic_index_in_dim(spectrum, index, 1, keepdims=False)
        real_out = jnp.dot(spec_here[0], wave_here[0], preferred_element_type=jnp.float32) + jnp.dot(spec_here[1], wave_here[1], preferred_element_type=jnp.float32)
        imag_out = jnp.dot(spec_here[1], wave_here[0], preferred_element_type=jnp.float32) - jnp.dot(spec_here[0], wave_here[1], preferred_element_type=jnp.float32)
        return jnp.stack([real_out, imag_out])
    result = lax.map(per_frequency, jnp.arange(F, dtype=jnp.int32))
    result = jnp.moveaxis(result, 0, 1).reshape(2, F, VS * S)
    return from_spectrum(result, table)

def norm_of(field):
    return jnp.sqrt(jnp.sum(field * field) + epsilon)

def reference(wave, observed):
    table = transform_tables()
    beta = norm_of(observed)
    data_vector = observed / beta
    model_vector = adjoint_op(data_vector, wave, table)
    alpha = norm_of(model_vector)
    model_vector = model_vector / alpha
    direction = model_vector
    solution = jnp.zeros_like(model_vector)
    phi_bar = beta
    rho_bar = alpha
    for step in range(ITERS):
        data_vector = forward_op(model_vector, wave, table) - alpha * data_vector
        beta = norm_of(data_vector)
        data_vector = data_vector / beta
        model_vector = adjoint_op(data_vector, wave, table) - beta * model_vector
        alpha = norm_of(model_vector)
        model_vector = model_vector / alpha
        rho_new = jnp.sqrt(rho_bar * rho_bar + beta * beta)
        cosine = rho_bar / rho_new
        sine_part = beta / rho_new
        theta = sine_part * alpha
        rho_bar = -cosine * alpha
        phi_value = cosine * phi_bar
        phi_bar = sine_part * phi_bar
        solution = solution + phi_value / rho_new * direction
        direction = model_vector - theta / rho_new * direction
    return solution
```

```python
import math

import jax
import jax.numpy as jnp
from jax import lax
from jax.sharding import PartitionSpec as P

VS = 16
ITERS = 3
SCALE = 0.5

precise = lax.Precision.HIGHEST
epsilon = 1e-06


def transform_tables(freq_total, samples):
    freq_index = lax.broadcasted_iota(jnp.int32, (freq_total, samples), 0) + 1
    time_index = lax.broadcasted_iota(jnp.int32, (freq_total, samples), 1)
    phases = (freq_index * time_index % samples).astype(jnp.float32) * (2.0 * math.pi / samples)
    factor = math.sqrt(2.0 / samples)
    return jnp.stack([factor * jnp.cos(phases), -factor * jnp.sin(phases)])


def two_parts(field):
    high = lax.reduce_precision(field, 8, 7)
    return jnp.concatenate([high, field - high]).astype(jnp.bfloat16)


def forward_product(model, wave):
    rows = two_parts(model.reshape(2 * VS, -1))

    def product_of(right):
        both = lax.dot_general(
            rows, right, (((1,), (1,)), ((), ())), preferred_element_type=jnp.float32
        )
        return both[: 2 * VS] + both[2 * VS :]

    by_real, by_imag = product_of(wave[0]), product_of(wave[1])
    return SCALE * jnp.stack([by_real[:VS] - by_imag[VS:], by_imag[:VS] + by_real[VS:]])


def adjoint_product(rows, wave):

    def product_of(right):
        both = jnp.dot(rows, right, preferred_element_type=jnp.float32)
        return both if rows.shape[0] == 2 * VS else both[: 2 * VS] + both[2 * VS :]

    by_real, by_imag = product_of(wave[0]), product_of(wave[1])
    return SCALE * jnp.stack([by_real[:VS] + by_imag[VS:], by_real[VS:] - by_imag[:VS]])


def iterate_weights(data_square, moments):
    model_norms = [jnp.sqrt(moments[2 * k]) for k in range(ITERS)]
    data_norms = [jnp.sqrt(data_square)] + [jnp.sqrt(moments[2 * k + 1]) for k in range(ITERS)]

    def ratio(top, bottom):
        return jnp.where(bottom > 0, top / jnp.where(bottom > 0, bottom, 1.0), 0.0)

    model_gram = [
        [ratio(ratio(moments[i + j], model_norms[i]), model_norms[j]) for j in range(ITERS)]
        for i in range(ITERS)
    ]

    def data_inner(i, j):
        low, high = min(i, j), max(i, j)
        if high == 0:
            return data_square
        if low == 0:
            return moments[high - 1]
        return moments[low + high - 1]

    data_gram = [
        [ratio(ratio(data_inner(i, j), data_norms[i]), data_norms[j]) for j in range(ITERS + 1)]
        for i in range(ITERS + 1)
    ]

    def norm_of(weights, gram):
        total = 0.0
        for i in range(len(weights)):
            total += weights[i] * weights[i] * ratio(gram[i][i], gram[i][i])
            for j in range(i):
                total += 2.0 * weights[i] * weights[j] * gram[i][j]
        return jnp.sqrt(jnp.maximum(total, 0.0) + epsilon)

    up = [ratio(data_norms[k + 1], model_norms[k]) / SCALE for k in range(ITERS)]
    down = [ratio(model_norms[k], data_norms[k]) / SCALE for k in range(ITERS)]
    zero = jnp.zeros_like(data_square)
    beta = jnp.sqrt(data_square + epsilon)
    data_vector = [data_norms[0] / beta] + [zero] * ITERS
    model_vector = [data_vector[k] * down[k] for k in range(ITERS)]
    alpha = norm_of(model_vector, model_gram)
    model_vector = [weight / alpha for weight in model_vector]
    direction = model_vector
    solution = [zero] * ITERS
    phi_bar = beta
    rho_bar = alpha
    for step in range(ITERS):
        image = [zero] + [model_vector[k] * up[k] for k in range(ITERS)]
        data_vector = [new - alpha * old for new, old in zip(image, data_vector)]
        beta = norm_of(data_vector, data_gram)
        data_vector = [weight / beta for weight in data_vector]
        rho_new = jnp.sqrt(rho_bar * rho_bar + beta * beta)
        cosine = rho_bar / rho_new
        sine_part = beta / rho_new
        phi_value = cosine * phi_bar
        phi_bar = sine_part * phi_bar
        solution = [
            old + phi_value / rho_new * weight for old, weight in zip(solution, direction)
        ]
        if step < ITERS - 1:
            image = [data_vector[k] * down[k] for k in range(ITERS)]
            model_vector = [new - beta * old for new, old in zip(image, model_vector)]
            alpha = norm_of(model_vector, model_gram)
            model_vector = [weight / alpha for weight in model_vector]
            theta = sine_part * alpha
            rho_bar = -cosine * alpha
            direction = [
                weight - theta / rho_new * old for weight, old in zip(model_vector, direction)
            ]
    return [ratio(weight, norm) for weight, norm in zip(solution, model_norms)]


def on_device(wave, observed):
    wave = wave[:, 0]
    panel_rows, sources = wave.shape[1:]
    blocks = lax.axis_size("freq")
    panels = lax.axis_size("panel")
    samples = observed.shape[2]
    table = transform_tables(blocks, samples)
    data = observed[0]

    def exchange(lines):
        return lax.all_to_all(lines, "freq", split_axis=0, concat_axis=0, tiled=True)

    lines = jnp.einsum("cft,rt->fcr", table, data, precision=precise).astype(jnp.bfloat16)
    moved_in = exchange(lines.reshape(-1)).reshape(blocks, 2, -1)
    rows = moved_in.transpose(1, 0, 2).reshape(2 * VS, panel_rows)

    bases, squares = [], [jnp.sum(data * data)]
    for step in range(ITERS):
        model = lax.psum(adjoint_product(rows, wave), "panel")
        image = forward_product(model, wave)
        bases.append(model)
        squares += [jnp.sum(model * model) / panels, jnp.sum(image * image)]
        rows = two_parts(image.reshape(2 * VS, -1))
    squares = lax.psum(jnp.stack(squares), ("freq", "panel"))
    weights = iterate_weights(squares[0], [squares[1 + k] for k in range(2 * ITERS)])
    spectrum = sum(weight * basis for weight, basis in zip(weights, bases))
    spectrum = spectrum.astype(jnp.bfloat16).reshape(2, blocks, -1)
    moved = exchange(spectrum.transpose(1, 0, 2).reshape(-1)).reshape(blocks, 2, -1)
    return jnp.einsum("jcr,cjt->rt", moved.astype(jnp.float32), table, precision=precise)


def solution(mesh):
    placed = (P(None, "freq", "panel", None), P("panel", "freq", None))
    return jax.shard_map(
        on_device, mesh=mesh, in_specs=placed, out_specs=P("freq", None), check_vma=False
    )
```

```python
import functools
import math

import jax
import jax.numpy as jnp
from jax import lax
from jax.experimental import pallas as pl
from jax.experimental.pallas import tpu as pltpu
from jax.sharding import PartitionSpec as P

VS = 16
ITERS = 3
SCALE = 0.5
NEAR = 16
GROUP = 8
MESH = pl.DeviceIdType.MESH

precise = lax.Precision.HIGHEST
epsilon = 1e-06


def transform_tables(freq_total, samples):
    freq_index = lax.broadcasted_iota(jnp.int32, (freq_total, samples), 0) + 1
    time_index = lax.broadcasted_iota(jnp.int32, (freq_total, samples), 1)
    phases = (freq_index * time_index % samples).astype(jnp.float32) * (2.0 * math.pi / samples)
    factor = math.sqrt(2.0 / samples)
    return jnp.stack([factor * jnp.cos(phases), -factor * jnp.sin(phases)])


def two_parts(field):
    high = field.astype(jnp.bfloat16)
    low = (field - high.astype(jnp.float32)).astype(jnp.bfloat16)
    return jnp.concatenate([high, low])


def product_of(rows, right, side):
    both = lax.dot_general(
        rows, right, (((1,), (side,)), ((), ())), preferred_element_type=jnp.float32
    )
    return both if rows.shape[0] == 2 * VS else both[: 2 * VS] + both[2 * VS :]


def iterate_weights(data_square, moments):
    model_norms = [jnp.sqrt(moments[2 * k]) for k in range(ITERS)]
    data_norms = [jnp.sqrt(data_square)] + [jnp.sqrt(moments[2 * k + 1]) for k in range(ITERS)]

    def ratio(top, bottom):
        return jnp.where(bottom > 0, top / jnp.where(bottom > 0, bottom, 1.0), 0.0)

    model_gram = [
        [ratio(ratio(moments[i + j], model_norms[i]), model_norms[j]) for j in range(ITERS)]
        for i in range(ITERS)
    ]

    def data_inner(i, j):
        low, high = min(i, j), max(i, j)
        if high == 0:
            return data_square
        if low == 0:
            return moments[high - 1]
        return moments[low + high - 1]

    data_gram = [
        [ratio(ratio(data_inner(i, j), data_norms[i]), data_norms[j]) for j in range(ITERS + 1)]
        for i in range(ITERS + 1)
    ]

    def norm_of(weights, gram):
        total = 0.0
        for i in range(len(weights)):
            total += weights[i] * weights[i] * ratio(gram[i][i], gram[i][i])
            for j in range(i):
                total += 2.0 * weights[i] * weights[j] * gram[i][j]
        return jnp.sqrt(jnp.maximum(total, 0.0) + epsilon)

    up = [ratio(data_norms[k + 1], model_norms[k]) / SCALE for k in range(ITERS)]
    down = [ratio(model_norms[k], data_norms[k]) / SCALE for k in range(ITERS)]
    zero = jnp.zeros_like(data_square)
    beta = jnp.sqrt(data_square + epsilon)
    data_vector = [data_norms[0] / beta] + [zero] * ITERS
    model_vector = [data_vector[k] * down[k] for k in range(ITERS)]
    alpha = norm_of(model_vector, model_gram)
    model_vector = [weight / alpha for weight in model_vector]
    direction = model_vector
    solution = [zero] * ITERS
    phi_bar = beta
    rho_bar = alpha
    for step in range(ITERS):
        image = [zero] + [model_vector[k] * up[k] for k in range(ITERS)]
        data_vector = [new - alpha * old for new, old in zip(image, data_vector)]
        beta = norm_of(data_vector, data_gram)
        data_vector = [weight / beta for weight in data_vector]
        rho_new = jnp.sqrt(rho_bar * rho_bar + beta * beta)
        cosine = rho_bar / rho_new
        sine_part = beta / rho_new
        phi_value = cosine * phi_bar
        phi_bar = sine_part * phi_bar
        solution = [
            old + phi_value / rho_new * weight for old, weight in zip(solution, direction)
        ]
        if step < ITERS - 1:
            image = [data_vector[k] * down[k] for k in range(ITERS)]
            model_vector = [new - beta * old for new, old in zip(image, model_vector)]
            alpha = norm_of(model_vector, model_gram)
            model_vector = [weight / alpha for weight in model_vector]
            theta = sine_part * alpha
            rho_bar = -cosine * alpha
            direction = [
                weight - theta / rho_new * old for weight, old in zip(model_vector, direction)
            ]
    return [ratio(weight, norm) for weight, norm in zip(solution, model_norms)]


def square_of(field):
    return jnp.broadcast_to(jnp.sum(field * field, keepdims=True), (1, 128))


def lsqr_kernel(
    panels,
    blocks,
    lines_ref,
    wave_ref,
    square_ref,
    spectrum_ref,
    parts,
    arrived,
    bases,
    sums,
    near,
    far,
    across,
    part_send,
    part_recv,
    base_send,
    base_recv,
    near_send,
    near_recv,
    far_send,
    far_recv,
    across_send,
    across_recv,
):
    me = lax.axis_index("panel")
    freq = lax.axis_index("freq")
    outer, inner = freq // NEAR, freq % NEAR
    distant = blocks // NEAR

    panel_peers = [{"panel": (me + k) % panels} for k in range(1, panels)]
    near_peers = [{"freq": outer * NEAR + (inner + k) % NEAR} for k in range(1, NEAR)]
    far_peers = [{"freq": (outer + k) % distant * NEAR + inner} for k in range(1, distant)]

    barrier = pltpu.get_barrier_semaphore()
    for peer in panel_peers + near_peers + far_peers:
        pl.semaphore_signal(barrier, inc=1, device_id=peer, device_id_type=MESH)

    sent = []

    def copy_to(peer, source, target, send_sem, recv_sem):
        copy = pltpu.make_async_remote_copy(
            src_ref=source,
            dst_ref=target,
            send_sem=send_sem,
            recv_sem=recv_sem,
            device_id=peer,
            device_id_type=MESH,
        )
        copy.start()
        sent.append(copy)

    def arrival(ref, recv_sem):
        pltpu.make_async_copy(ref, ref, recv_sem).wait()

    sums[...] = jnp.zeros_like(sums)
    sums[0:1, :] = square_ref[...]
    rows = lines_ref[...]
    for step in range(ITERS):
        by_real = product_of(rows, wave_ref[0], 0)
        by_imag = product_of(rows, wave_ref[1], 0)
        real_part = SCALE * (by_real[:VS] + by_imag[VS:])
        imag_part = SCALE * (by_real[VS:] - by_imag[:VS])
        parts[step, : panels // 2] = real_part.reshape(panels // 2, GROUP, -1)
        parts[step, panels // 2 :] = imag_part.reshape(panels // 2, GROUP, -1)
        if step == 0:
            pl.semaphore_wait(barrier, len(panel_peers + near_peers + far_peers))
        for k in range(1, panels):
            copy_to(
                panel_peers[k - 1],
                parts.at[step, (me + k) % panels],
                arrived.at[step, k - 1],
                part_send.at[step, k - 1],
                part_recv.at[step, k - 1],
            )
        total = parts[step, me]
        for k in range(1, panels):
            arrival(arrived.at[step, k - 1], part_recv.at[step, k - 1])
            total = total + arrived[step, k - 1]
        bases[step, me] = total
        for k in range(1, panels):
            copy_to(
                panel_peers[k - 1],
                bases.at[step, me],
                bases.at[step, me],
                base_send.at[step, k - 1],
                base_recv.at[step, k - 1],
            )
        sums[2 * step + 1 : 2 * step + 2, :] = square_of(total)
        for k in range(1, panels):
            arrival(bases.at[step, (me + panels - k) % panels], base_recv.at[step, k - 1])
        model_rows = two_parts(bases[step].reshape(2 * VS, -1))
        by_real = product_of(model_rows, wave_ref[0], 1)
        by_imag = product_of(model_rows, wave_ref[1], 1)
        image = SCALE * jnp.concatenate(
            [by_real[:VS] - by_imag[VS:], by_imag[:VS] + by_real[VS:]]
        )
        sums[2 * step + 2 : 2 * step + 3, :] = square_of(image)
        if step < ITERS - 1:
            rows = two_parts(image)

    def summed(value, held, count, index, peers, send_sem, recv_sem):
        held[index] = value
        for k in range(1, count):
            copy_to(
                peers[k - 1],
                held.at[index],
                held.at[index],
                send_sem.at[k - 1],
                recv_sem.at[k - 1],
            )
        for k in range(1, count):
            arrival(held.at[(index + count - k) % count], recv_sem.at[k - 1])
        return jnp.sum(held[...], axis=0)

    value = summed(sums[...], near, NEAR, inner, near_peers, near_send, near_recv)
    value = summed(value, far, distant, outer, far_peers, far_send, far_recv)
    value = summed(value, across, panels, me, panel_peers, across_send, across_recv)
    squares = [value[k : k + 1, :] for k in range(2 * ITERS + 1)]
    weights = iterate_weights(squares[0], squares[1:])
    spectrum = sum(
        weight[:, :1] * bases[step].reshape(2 * VS, -1) for step, weight in enumerate(weights)
    )
    spectrum_ref[...] = spectrum.astype(jnp.bfloat16)
    for copy in sent:
        copy.wait_send()


def solved_spectrum(lines, wave, square, panels, blocks):
    sources = wave.shape[2]
    quarter = (GROUP, sources)
    tile = (8, 128)
    distant = blocks // NEAR
    dma = pltpu.SemaphoreType.DMA
    return pl.pallas_call(
        functools.partial(lsqr_kernel, panels, blocks),
        out_shape=jax.ShapeDtypeStruct((2 * VS, sources), jnp.bfloat16),
        in_specs=[pl.BlockSpec(memory_space=pltpu.VMEM)] * 3,
        out_specs=pl.BlockSpec(memory_space=pltpu.VMEM),
        scratch_shapes=[
            pltpu.VMEM((ITERS, panels, *quarter), jnp.float32),
            pltpu.VMEM((ITERS, panels - 1, *quarter), jnp.float32),
            pltpu.VMEM((ITERS, panels, *quarter), jnp.float32),
            pltpu.VMEM(tile, jnp.float32),
            pltpu.VMEM((NEAR, *tile), jnp.float32),
            pltpu.VMEM((distant, *tile), jnp.float32),
            pltpu.VMEM((panels, *tile), jnp.float32),
            dma((ITERS, panels - 1)),
            dma((ITERS, panels - 1)),
            dma((ITERS, panels - 1)),
            dma((ITERS, panels - 1)),
            dma((NEAR - 1,)),
            dma((NEAR - 1,)),
            dma((distant - 1,)),
            dma((distant - 1,)),
            dma((panels - 1,)),
            dma((panels - 1,)),
        ],
        compiler_params=pltpu.CompilerParams(
            collective_id=0, has_side_effects=True, vmem_limit_bytes=32 * 1024 * 1024
        ),
    )(lines, wave, square)


def on_device(wave, observed):
    wave = wave[:, 0]
    panel_rows = wave.shape[1]
    blocks = lax.axis_size("freq")
    panels = lax.axis_size("panel")
    table = transform_tables(blocks, observed.shape[2])
    data = observed[0]

    def exchange(lines):
        moved = lax.all_to_all(lines.reshape(-1), "freq", split_axis=0, concat_axis=0, tiled=True)
        return moved.reshape(blocks, 2, -1)

    lines = jnp.einsum("cft,rt->fcr", table, data, precision=precise).astype(jnp.bfloat16)
    rows = exchange(lines).transpose(1, 0, 2).reshape(2 * VS, panel_rows)
    square = jnp.full((1, 128), jnp.sum(data * data))
    spectrum = solved_spectrum(rows, wave, square, panels, blocks).reshape(2, blocks, -1)
    moved = exchange(spectrum.transpose(1, 0, 2))
    return jnp.einsum("jcr,cjt->rt", moved.astype(jnp.float32), table, precision=precise)


def solution(mesh):
    placed = (P(None, "freq", "panel", None), P("panel", "freq", None))
    return jax.shard_map(
        on_device, mesh=mesh, in_specs=placed, out_specs=P("freq", None), check_vma=False
    )
```

```python
import functools
import math

import jax
import jax.numpy as jnp
from jax import lax
from jax.experimental import pallas as pl
from jax.experimental.pallas import tpu as pltpu
from jax.sharding import PartitionSpec as P

VS = 16
ITERS = 3
SCALE = 0.5
NEAR = 16
GROUP = 8
LANES = 128
MESH = pl.DeviceIdType.MESH

precise = lax.Precision.HIGHEST
epsilon = 1e-06


def transform_tables(freq_total, samples):
    freq_index = lax.broadcasted_iota(jnp.int32, (freq_total, samples), 0) + 1
    time_index = lax.broadcasted_iota(jnp.int32, (freq_total, samples), 1)
    phases = (freq_index * time_index % samples).astype(jnp.float32) * (2.0 * math.pi / samples)
    factor = math.sqrt(2.0 / samples)
    return jnp.stack([factor * jnp.cos(phases), -factor * jnp.sin(phases)])


def two_parts(field):
    high = field.astype(jnp.bfloat16)
    low = (field - high.astype(jnp.float32)).astype(jnp.bfloat16)
    return jnp.concatenate([high, low])


def product_of(rows, right, side):
    both = lax.dot_general(
        rows, right, (((1,), (side,)), ((), ())), preferred_element_type=jnp.float32
    )
    return both if rows.shape[0] == 2 * VS else both[: 2 * VS] + both[2 * VS :]


def iterate_weights(data_square, moments):
    model_norms = [jnp.sqrt(moments[2 * k]) for k in range(ITERS)]
    data_norms = [jnp.sqrt(data_square)] + [jnp.sqrt(moments[2 * k + 1]) for k in range(ITERS)]

    def ratio(top, bottom):
        return jnp.where(bottom > 0, top / jnp.where(bottom > 0, bottom, 1.0), 0.0)

    model_gram = [
        [ratio(ratio(moments[i + j], model_norms[i]), model_norms[j]) for j in range(ITERS)]
        for i in range(ITERS)
    ]

    def data_inner(i, j):
        low, high = min(i, j), max(i, j)
        if high == 0:
            return data_square
        if low == 0:
            return moments[high - 1]
        return moments[low + high - 1]

    data_gram = [
        [ratio(ratio(data_inner(i, j), data_norms[i]), data_norms[j]) for j in range(ITERS + 1)]
        for i in range(ITERS + 1)
    ]

    def norm_of(weights, gram):
        total = 0.0
        for i in range(len(weights)):
            total += weights[i] * weights[i] * ratio(gram[i][i], gram[i][i])
            for j in range(i):
                total += 2.0 * weights[i] * weights[j] * gram[i][j]
        return jnp.sqrt(jnp.maximum(total, 0.0) + epsilon)

    up = [ratio(data_norms[k + 1], model_norms[k]) / SCALE for k in range(ITERS)]
    down = [ratio(model_norms[k], data_norms[k]) / SCALE for k in range(ITERS)]
    zero = jnp.zeros_like(data_square)
    beta = jnp.sqrt(data_square + epsilon)
    data_vector = [data_norms[0] / beta] + [zero] * ITERS
    model_vector = [data_vector[k] * down[k] for k in range(ITERS)]
    alpha = norm_of(model_vector, model_gram)
    model_vector = [weight / alpha for weight in model_vector]
    direction = model_vector
    solution = [zero] * ITERS
    phi_bar = beta
    rho_bar = alpha
    for step in range(ITERS):
        image = [zero] + [model_vector[k] * up[k] for k in range(ITERS)]
        data_vector = [new - alpha * old for new, old in zip(image, data_vector)]
        beta = norm_of(data_vector, data_gram)
        data_vector = [weight / beta for weight in data_vector]
        rho_new = jnp.sqrt(rho_bar * rho_bar + beta * beta)
        cosine = rho_bar / rho_new
        sine_part = beta / rho_new
        phi_value = cosine * phi_bar
        phi_bar = sine_part * phi_bar
        solution = [
            old + phi_value / rho_new * weight for old, weight in zip(solution, direction)
        ]
        if step < ITERS - 1:
            image = [data_vector[k] * down[k] for k in range(ITERS)]
            model_vector = [new - beta * old for new, old in zip(image, model_vector)]
            alpha = norm_of(model_vector, model_gram)
            model_vector = [weight / alpha for weight in model_vector]
            theta = sine_part * alpha
            rho_bar = -cosine * alpha
            direction = [
                weight - theta / rho_new * old for weight, old in zip(model_vector, direction)
            ]
    return [ratio(weight, norm) for weight, norm in zip(solution, model_norms)]


def square_of(field):
    return jnp.broadcast_to(jnp.sum(field * field, keepdims=True), (1, 128))


def lsqr_kernel(
    panels,
    blocks,
    lines_ref,
    wave_ref,
    square_ref,
    spectrum_ref,
    lines_in,
    data_rows,
    leaving,
    landed,
    parts,
    arrived,
    bases,
    sums,
    near,
    far,
    across,
    lines_send,
    lines_recv,
    trace_send,
    trace_recv,
    part_send,
    part_recv,
    base_send,
    base_recv,
    near_send,
    near_recv,
    far_send,
    far_recv,
    across_send,
    across_recv,
):
    me = lax.axis_index("panel")
    freq = lax.axis_index("freq")
    outer, inner = freq // NEAR, freq % NEAR
    distant = blocks // NEAR

    panel_peers = [{"panel": (me + k) % panels} for k in range(1, panels)]
    near_peers = [{"freq": outer * NEAR + (inner + k) % NEAR} for k in range(1, NEAR)]
    far_peers = [{"freq": (outer + k) % distant * NEAR + inner} for k in range(1, distant)]

    barrier = pltpu.get_barrier_semaphore()
    for peer in panel_peers:
        pl.semaphore_signal(barrier, inc=1, device_id=peer, device_id_type=MESH)

    @pl.loop(1, blocks)
    def _(k):
        peer = {"freq": (freq + k) % blocks}
        pl.semaphore_signal(barrier, inc=1, device_id=peer, device_id_type=MESH)

    strips = blocks // VS
    chunk = bases.shape[-1] // strips
    half = leaving.shape[-1] // 2
    span = data_rows.shape[-1] // strips

    def slot_of(index):
        return index % strips * VS + index // strips

    sent = []

    def copy_to(peer, source, target, send_sem, recv_sem):
        copy = pltpu.make_async_remote_copy(
            src_ref=source,
            dst_ref=target,
            send_sem=send_sem,
            recv_sem=recv_sem,
            device_id=peer,
            device_id_type=MESH,
        )
        copy.start()
        sent.append(copy)

    def arrival(ref, recv_sem):
        pltpu.make_async_copy(ref, ref, recv_sem).wait()

    def exchange(source, source_slot, target, target_slot, send_sem, recv_sem):
        target[target_slot(freq)] = source[source_slot(freq)]

        @pl.loop(1, blocks)
        def _(k):
            peer = (freq + k) % blocks
            pltpu.make_async_remote_copy(
                src_ref=source.at[source_slot(peer)],
                dst_ref=target.at[target_slot(freq)],
                send_sem=send_sem,
                recv_sem=recv_sem,
                device_id={"freq": peer},
                device_id_type=MESH,
            ).start()

    def exchanged(ref, sem):
        others = ref.at[pl.ds(0, blocks - 1)]
        pltpu.make_async_copy(others, others, sem).wait()

    def same(index):
        return index

    def send_traces(step):
        model = bases[step].reshape(2 * VS, -1)
        for strip in range(strips):
            columns = slice(strip * chunk, (strip + 1) * chunk)
            slots = slice(strip * VS, (strip + 1) * VS)
            leaving[step, slots, 0, :chunk] = model[:VS, columns]
            leaving[step, slots, 0, half : half + chunk] = model[VS:, columns]
        exchange(
            leaving.at[step],
            slot_of,
            landed.at[step],
            same,
            trace_send.at[step],
            trace_recv.at[step],
        )

    leaving[...] = jnp.zeros_like(leaving)
    sums[...] = jnp.zeros_like(sums)
    sums[0:1, :] = square_ref[...]
    pl.semaphore_wait(barrier, len(panel_peers) + blocks - 1)
    exchange(lines_ref, same, lines_in, slot_of, lines_send, lines_recv)
    exchanged(lines_in, lines_recv)
    for strip in range(strips):
        columns = slice(strip * span, (strip + 1) * span)
        slots = slice(strip * VS, (strip + 1) * VS)
        data_rows[:VS, columns] = lines_in[slots, 0, :span]
        data_rows[VS:, columns] = lines_in[slots, 0, LANES // 2 : LANES // 2 + span]
    rows = two_parts(data_rows[...])
    for step in range(ITERS):
        by_real = product_of(rows, wave_ref[0], 0)
        by_imag = product_of(rows, wave_ref[1], 0)
        real_part = SCALE * (by_real[:VS] + by_imag[VS:])
        imag_part = SCALE * (by_real[VS:] - by_imag[:VS])
        parts[step, : panels // 2] = real_part.reshape(panels // 2, GROUP, -1)
        parts[step, panels // 2 :] = imag_part.reshape(panels // 2, GROUP, -1)
        for k in range(1, panels):
            copy_to(
                panel_peers[k - 1],
                parts.at[step, (me + k) % panels],
                arrived.at[step, k - 1],
                part_send.at[step, k - 1],
                part_recv.at[step, k - 1],
            )
        if step > 0:
            send_traces(step - 1)
        total = parts[step, me]
        for k in range(1, panels):
            arrival(arrived.at[step, k - 1], part_recv.at[step, k - 1])
            total = total + arrived[step, k - 1]
        bases[step, me] = total
        for k in range(1, panels):
            copy_to(
                panel_peers[k - 1],
                bases.at[step, me],
                bases.at[step, me],
                base_send.at[step, k - 1],
                base_recv.at[step, k - 1],
            )
        sums[2 * step + 1 : 2 * step + 2, :] = square_of(total)
        for k in range(1, panels):
            arrival(bases.at[step, (me + panels - k) % panels], base_recv.at[step, k - 1])
        model_rows = two_parts(bases[step].reshape(2 * VS, -1))
        by_real = product_of(model_rows, wave_ref[0], 1)
        by_imag = product_of(model_rows, wave_ref[1], 1)
        image = SCALE * jnp.concatenate(
            [by_real[:VS] - by_imag[VS:], by_imag[:VS] + by_real[VS:]]
        )
        sums[2 * step + 2 : 2 * step + 3, :] = square_of(image)
        if step < ITERS - 1:
            rows = two_parts(image)

    def summed(value, held, count, index, peers, send_sem, recv_sem, meanwhile=None):
        held[index] = value
        for k in range(1, count):
            copy_to(
                peers[k - 1],
                held.at[index],
                held.at[index],
                send_sem.at[k - 1],
                recv_sem.at[k - 1],
            )
        if meanwhile is not None:
            meanwhile()
        for k in range(1, count):
            arrival(held.at[(index + count - k) % count], recv_sem.at[k - 1])
        return jnp.sum(held[...], axis=0)

    value = summed(
        sums[...],
        near,
        NEAR,
        inner,
        near_peers,
        near_send,
        near_recv,
        lambda: send_traces(ITERS - 1),
    )
    value = summed(value, far, distant, outer, far_peers, far_send, far_recv)
    value = summed(value, across, panels, me, panel_peers, across_send, across_recv)
    squares = [value[k : k + 1, :] for k in range(2 * ITERS + 1)]
    weights = iterate_weights(squares[0], squares[1:])
    for step in range(ITERS):
        exchanged(landed.at[step], trace_recv.at[step])
    spectrum_ref[...] = sum(
        weight[:, :1].reshape(1, 1, 1) * landed[step] for step, weight in enumerate(weights)
    )
    for copy in sent:
        copy.wait_send()
    exchanged(lines_in, lines_send)
    for step in range(ITERS):
        exchanged(landed.at[step], trace_send.at[step])


def solved_spectra(lines, wave, square, panels, blocks):
    sources = wave.shape[2]
    quarter = (GROUP, sources)
    tile = (8, LANES)
    distant = blocks // NEAR
    half = -(-2 * VS * sources // (2 * blocks) // LANES) * LANES
    dma = pltpu.SemaphoreType.DMA
    return pl.pallas_call(
        functools.partial(lsqr_kernel, panels, blocks),
        out_shape=jax.ShapeDtypeStruct((blocks, 1, 2 * half), jnp.float32),
        in_specs=[pl.BlockSpec(memory_space=pltpu.VMEM)] * 3,
        out_specs=pl.BlockSpec(memory_space=pltpu.VMEM),
        scratch_shapes=[
            pltpu.VMEM((blocks, 1, LANES), jnp.float32),
            pltpu.VMEM((2 * VS, wave.shape[1]), jnp.float32),
            pltpu.VMEM((ITERS, blocks, 1, 2 * half), jnp.float32),
            pltpu.VMEM((ITERS, blocks, 1, 2 * half), jnp.float32),
            pltpu.VMEM((ITERS, panels, *quarter), jnp.float32),
            pltpu.VMEM((ITERS, panels - 1, *quarter), jnp.float32),
            pltpu.VMEM((ITERS, panels, *quarter), jnp.float32),
            pltpu.VMEM(tile, jnp.float32),
            pltpu.VMEM((NEAR, *tile), jnp.float32),
            pltpu.VMEM((distant, *tile), jnp.float32),
            pltpu.VMEM((panels, *tile), jnp.float32),
            dma,
            dma,
            dma((ITERS,)),
            dma((ITERS,)),
            dma((ITERS, panels - 1)),
            dma((ITERS, panels - 1)),
            dma((ITERS, panels - 1)),
            dma((ITERS, panels - 1)),
            dma((NEAR - 1,)),
            dma((NEAR - 1,)),
            dma((distant - 1,)),
            dma((distant - 1,)),
            dma((panels - 1,)),
            dma((panels - 1,)),
        ],
        compiler_params=pltpu.CompilerParams(
            collective_id=0, has_side_effects=True, vmem_limit_bytes=32 * 1024 * 1024
        ),
    )(lines, wave, square)


def on_device(wave, observed):
    wave = wave[:, 0]
    blocks = lax.axis_size("freq")
    panels = lax.axis_size("panel")
    table = transform_tables(blocks, observed.shape[2])
    data = observed[0]

    lines = jnp.einsum("cft,rt->fcr", table, data, precision=precise)
    lines = jnp.pad(lines, ((0, 0), (0, 0), (0, LANES // 2 - data.shape[0])))
    square = jnp.full((1, LANES), jnp.sum(data * data))
    spectra = solved_spectra(lines.reshape(blocks, 1, LANES), wave, square, panels, blocks)
    spectra = spectra.reshape(blocks, 2, -1)[:, :, : VS * wave.shape[2] // blocks]
    return jnp.einsum("jcr,cjt->rt", spectra, table, precision=precise)


def solution(mesh):
    placed = (P(None, "freq", "panel", None), P("panel", "freq", None))
    return jax.shard_map(
        on_device, mesh=mesh, in_specs=placed, out_specs=P("freq", None), check_vma=False
    )
```

```python
import functools
import math

import jax
import jax.numpy as jnp
import numpy as np
from jax import lax
from jax.experimental import pallas as pl
from jax.experimental.pallas import tpu as pltpu
from jax.sharding import PartitionSpec as P

VS = 16
ITERS = 3
SCALE = 0.5
GROUP = 8
LANES = 128
MESH = pl.DeviceIdType.MESH

precise = lax.Precision.HIGHEST
epsilon = 1e-06


def transform_tables(freq_total, samples):
    freq_index = np.arange(freq_total)[:, None] + 1
    time_index = np.arange(samples)[None, :]
    phases = (freq_index * time_index % samples) * (2.0 * math.pi / samples)
    factor = math.sqrt(2.0 / samples)
    return np.stack([factor * np.cos(phases), -factor * np.sin(phases)]).astype(np.float32)


def two_parts(field):
    high = field.astype(jnp.bfloat16)
    low = (field - high.astype(jnp.float32)).astype(jnp.bfloat16)
    return jnp.concatenate([high, low])


def product_of(rows, right, side):
    both = lax.dot_general(
        rows, right, (((1,), (side,)), ((), ())), preferred_element_type=jnp.float32
    )
    return both if rows.shape[0] == 2 * VS else both[: 2 * VS] + both[2 * VS :]


def iterate_weights(data_square, moments):
    model_norms = [jnp.sqrt(moments[2 * k]) for k in range(ITERS)]
    data_norms = [jnp.sqrt(data_square)] + [jnp.sqrt(moments[2 * k + 1]) for k in range(ITERS)]

    def ratio(top, bottom):
        return jnp.where(bottom > 0, top / jnp.where(bottom > 0, bottom, 1.0), 0.0)

    model_gram = [
        [ratio(ratio(moments[i + j], model_norms[i]), model_norms[j]) for j in range(ITERS)]
        for i in range(ITERS)
    ]

    def data_inner(i, j):
        low, high = min(i, j), max(i, j)
        if high == 0:
            return data_square
        if low == 0:
            return moments[high - 1]
        return moments[low + high - 1]

    data_gram = [
        [ratio(ratio(data_inner(i, j), data_norms[i]), data_norms[j]) for j in range(ITERS + 1)]
        for i in range(ITERS + 1)
    ]

    def norm_of(weights, gram):
        total = 0.0
        for i in range(len(weights)):
            total += weights[i] * weights[i] * ratio(gram[i][i], gram[i][i])
            for j in range(i):
                total += 2.0 * weights[i] * weights[j] * gram[i][j]
        return jnp.sqrt(jnp.maximum(total, 0.0) + epsilon)

    up = [ratio(data_norms[k + 1], model_norms[k]) / SCALE for k in range(ITERS)]
    down = [ratio(model_norms[k], data_norms[k]) / SCALE for k in range(ITERS)]
    zero = jnp.zeros_like(data_square)
    beta = jnp.sqrt(data_square + epsilon)
    data_vector = [data_norms[0] / beta] + [zero] * ITERS
    model_vector = [data_vector[k] * down[k] for k in range(ITERS)]
    alpha = norm_of(model_vector, model_gram)
    model_vector = [weight / alpha for weight in model_vector]
    direction = model_vector
    solution = [zero] * ITERS
    phi_bar = beta
    rho_bar = alpha
    for step in range(ITERS):
        image = [zero] + [model_vector[k] * up[k] for k in range(ITERS)]
        data_vector = [new - alpha * old for new, old in zip(image, data_vector)]
        beta = norm_of(data_vector, data_gram)
        data_vector = [weight / beta for weight in data_vector]
        rho_new = jnp.sqrt(rho_bar * rho_bar + beta * beta)
        cosine = rho_bar / rho_new
        sine_part = beta / rho_new
        phi_value = cosine * phi_bar
        phi_bar = sine_part * phi_bar
        solution = [
            old + phi_value / rho_new * weight for old, weight in zip(solution, direction)
        ]
        if step < ITERS - 1:
            image = [data_vector[k] * down[k] for k in range(ITERS)]
            model_vector = [new - beta * old for new, old in zip(image, model_vector)]
            alpha = norm_of(model_vector, model_gram)
            model_vector = [weight / alpha for weight in model_vector]
            theta = sine_part * alpha
            rho_bar = -cosine * alpha
            direction = [
                weight - theta / rho_new * old for weight, old in zip(model_vector, direction)
            ]
    return [ratio(weight, norm) for weight, norm in zip(solution, model_norms)]


def square_of(field):
    return jnp.broadcast_to(jnp.sum(field * field, keepdims=True), (1, 128))


def lsqr_kernel(
    panels,
    blocks,
    data_hbm,
    table_hbm,
    wave_hbm,
    spectrum_ref,
    data_ref,
    table_ref,
    wave_ref,
    lines_out,
    lines_in,
    data_rows,
    leaving,
    landed,
    parts,
    arrived,
    bases,
    sums_out,
    sums_in,
    across,
    load_sem,
    lines_send,
    lines_recv,
    trace_send,
    trace_recv,
    part_send,
    part_recv,
    base_send,
    base_recv,
    sums_send,
    sums_recv,
    across_send,
    across_recv,
):
    me = lax.axis_index("panel")
    freq = lax.axis_index("freq")
    panel_peers = [{"panel": (me + k) % panels} for k in range(1, panels)]

    loads = [
        pltpu.make_async_copy(data_hbm, data_ref, load_sem.at[0]),
        pltpu.make_async_copy(table_hbm, table_ref, load_sem.at[1]),
        pltpu.make_async_copy(wave_hbm.at[:, 0], wave_ref, load_sem.at[2]),
    ]
    for load in loads:
        load.start()

    barrier = pltpu.get_barrier_semaphore()
    for peer in panel_peers:
        pl.semaphore_signal(barrier, inc=1, device_id=peer, device_id_type=MESH)

    @pl.loop(1, blocks)
    def _(k):
        peer = {"freq": (freq + k) % blocks}
        pl.semaphore_signal(barrier, inc=1, device_id=peer, device_id_type=MESH)

    strips = blocks // VS
    chunk = bases.shape[-1] // strips
    half = leaving.shape[-1] // 2
    span = data_rows.shape[-1] // strips

    def slot_of(index):
        return index % strips * VS + index // strips

    sent = []

    def copy_to(peer, source, target, send_sem, recv_sem):
        copy = pltpu.make_async_remote_copy(
            src_ref=source,
            dst_ref=target,
            send_sem=send_sem,
            recv_sem=recv_sem,
            device_id=peer,
            device_id_type=MESH,
        )
        copy.start()
        sent.append(copy)

    def arrival(ref, recv_sem):
        pltpu.make_async_copy(ref, ref, recv_sem).wait()

    def exchange(source, source_slot, target, target_slot, send_sem, recv_sem):
        target[target_slot(freq)] = source[source_slot(freq)]

        @pl.loop(1, blocks)
        def _(k):
            peer = (freq + k) % blocks
            pltpu.make_async_remote_copy(
                src_ref=source.at[source_slot(peer)],
                dst_ref=target.at[target_slot(freq)],
                send_sem=send_sem,
                recv_sem=recv_sem,
                device_id={"freq": peer},
                device_id_type=MESH,
            ).start()

    def exchanged(ref, sem):
        others = ref.at[pl.ds(0, blocks - 1)]
        pltpu.make_async_copy(others, others, sem).wait()

    def same(index):
        return index

    def send_traces(step):
        model = bases[step].reshape(2 * VS, -1)
        for strip in range(strips):
            columns = slice(strip * chunk, (strip + 1) * chunk)
            slots = slice(strip * VS, (strip + 1) * VS)
            leaving[step, slots, 0, :chunk] = model[:VS, columns]
            leaving[step, slots, 0, half : half + chunk] = model[VS:, columns]
        exchange(
            leaving.at[step],
            slot_of,
            landed.at[step],
            same,
            trace_send.at[step],
            trace_recv.at[step],
        )

    lanes = lax.broadcasted_iota(jnp.int32, (1, LANES), 1)
    lines_out[...] = jnp.zeros_like(lines_out)
    loads[0].wait()
    loads[1].wait()
    data = data_ref[:, 0, :]
    squares = [square_of(data)]
    for part in range(2):
        first = part * (LANES // 2)
        lines_out[:, 0, first : first + data.shape[0]] = lax.dot_general(
            table_ref[part], data, (((1,), (1,)), ((), ())), precision=precise
        )
    pl.semaphore_wait(barrier, len(panel_peers) + blocks - 1)
    exchange(lines_out, same, lines_in, slot_of, lines_send, lines_recv)
    leaving[...] = jnp.zeros_like(leaving)
    loads[2].wait()
    exchanged(lines_in, lines_recv)
    for strip in range(strips):
        columns = slice(strip * span, (strip + 1) * span)
        slots = slice(strip * VS, (strip + 1) * VS)
        data_rows[:VS, columns] = lines_in[slots, 0, :span]
        data_rows[VS:, columns] = lines_in[slots, 0, LANES // 2 : LANES // 2 + span]
    rows = two_parts(data_rows[...])
    for step in range(ITERS):
        by_real = product_of(rows, wave_ref[0], 0)
        by_imag = product_of(rows, wave_ref[1], 0)
        real_part = SCALE * (by_real[:VS] + by_imag[VS:])
        imag_part = SCALE * (by_real[VS:] - by_imag[:VS])
        parts[step, : panels // 2] = real_part.reshape(panels // 2, GROUP, -1)
        parts[step, panels // 2 :] = imag_part.reshape(panels // 2, GROUP, -1)
        for k in range(1, panels):
            copy_to(
                panel_peers[k - 1],
                parts.at[step, (me + k) % panels],
                arrived.at[step, k - 1],
                part_send.at[step, k - 1],
                part_recv.at[step, k - 1],
            )
        if step > 0:
            send_traces(step - 1)
        total = parts[step, me]
        for k in range(1, panels):
            arrival(arrived.at[step, k - 1], part_recv.at[step, k - 1])
            total = total + arrived[step, k - 1]
        bases[step, me] = total
        for k in range(1, panels):
            copy_to(
                panel_peers[k - 1],
                bases.at[step, me],
                bases.at[step, me],
                base_send.at[step, k - 1],
                base_recv.at[step, k - 1],
            )
        squares.append(square_of(total))
        for k in range(1, panels):
            arrival(bases.at[step, (me + panels - k) % panels], base_recv.at[step, k - 1])
        model_rows = two_parts(bases[step].reshape(2 * VS, -1))
        by_real = product_of(model_rows, wave_ref[0], 1)
        by_imag = product_of(model_rows, wave_ref[1], 1)
        image = SCALE * jnp.concatenate(
            [by_real[:VS] - by_imag[VS:], by_imag[:VS] + by_real[VS:]]
        )
        squares.append(square_of(image))
        if step < ITERS - 1:
            rows = two_parts(image)

    sums_out[0] = sum(
        jnp.where(lanes == k, square, 0.0) for k, square in enumerate(squares)
    )
    exchange(sums_out, lambda index: 0, sums_in, same, sums_send, sums_recv)
    send_traces(ITERS - 1)
    exchanged(sums_in, sums_recv)
    across[me] = jnp.sum(sums_in[...], axis=0)
    for k in range(1, panels):
        copy_to(
            panel_peers[k - 1],
            across.at[me],
            across.at[me],
            across_send.at[k - 1],
            across_recv.at[k - 1],
        )
    for k in range(1, panels):
        arrival(across.at[(me + panels - k) % panels], across_recv.at[k - 1])
    total = across[0]
    for k in range(1, panels):
        total = total + across[k]
    squares = [
        jnp.broadcast_to(jnp.sum(jnp.where(lanes == k, total, 0.0), keepdims=True), (1, LANES))
        for k in range(len(squares))
    ]
    weights = iterate_weights(squares[0], squares[1:])
    weights = [jnp.concatenate([weight] * (2 * half // LANES), axis=1) for weight in weights]
    for step in range(ITERS):
        exchanged(landed.at[step], trace_recv.at[step])
    for first in range(0, blocks, VS):
        rows = slice(first, first + VS)
        spectrum_ref[rows] = sum(
            weight[None] * landed[step, rows] for step, weight in enumerate(weights)
        )
    for copy in sent:
        copy.wait_send()
    exchanged(lines_in, lines_send)
    exchanged(sums_in, sums_send)
    for step in range(ITERS):
        exchanged(landed.at[step], trace_send.at[step])


def solved_spectra(data, table, wave, panels, blocks):
    sources = wave.shape[3]
    quarter = (GROUP, sources)
    row = (1, LANES)
    half = -(-2 * VS * sources // (2 * blocks) // LANES) * LANES
    dma = pltpu.SemaphoreType.DMA
    return pl.pallas_call(
        functools.partial(lsqr_kernel, panels, blocks),
        out_shape=jax.ShapeDtypeStruct((blocks, 1, 2 * half), jnp.float32),
        in_specs=[pl.BlockSpec(memory_space=pl.ANY)] * 3,
        out_specs=pl.BlockSpec(memory_space=pltpu.VMEM),
        scratch_shapes=[
            pltpu.VMEM(data.shape, jnp.float32),
            pltpu.VMEM(table.shape, jnp.float32),
            pltpu.VMEM((2, *wave.shape[2:]), jnp.bfloat16),
            pltpu.VMEM((blocks, *row), jnp.float32),
            pltpu.VMEM((blocks, *row), jnp.float32),
            pltpu.VMEM((2 * VS, wave.shape[2]), jnp.float32),
            pltpu.VMEM((ITERS, blocks, 1, 2 * half), jnp.float32),
            pltpu.VMEM((ITERS, blocks, 1, 2 * half), jnp.float32),
            pltpu.VMEM((ITERS, panels, *quarter), jnp.float32),
            pltpu.VMEM((ITERS, panels - 1, *quarter), jnp.float32),
            pltpu.VMEM((ITERS, panels, *quarter), jnp.float32),
            pltpu.VMEM((1, *row), jnp.float32),
            pltpu.VMEM((blocks, *row), jnp.float32),
            pltpu.VMEM((panels, *row), jnp.float32),
            dma((3,)),
            dma,
            dma,
            dma((ITERS,)),
            dma((ITERS,)),
            dma((ITERS, panels - 1)),
            dma((ITERS, panels - 1)),
            dma((ITERS, panels - 1)),
            dma((ITERS, panels - 1)),
            dma,
            dma,
            dma((panels - 1,)),
            dma((panels - 1,)),
        ],
        compiler_params=pltpu.CompilerParams(
            collective_id=0, has_side_effects=True, vmem_limit_bytes=63 * 1024 * 1024
        ),
    )(data, table, wave)


def on_device(wave, observed):
    blocks = lax.axis_size("freq")
    panels = lax.axis_size("panel")
    table = jnp.asarray(transform_tables(blocks, observed.shape[2]))
    traces = observed.transpose(1, 0, 2)
    spectra = solved_spectra(traces, table, wave, panels, blocks)
    spectra = spectra.reshape(blocks, 2, -1)[:, :, : VS * wave.shape[3] // blocks]
    return jnp.einsum("jcr,cjt->rt", spectra, table, precision=precise)


def solution(mesh):
    placed = (P(None, "freq", "panel", None), P("panel", "freq", None))
    return jax.shard_map(
        on_device, mesh=mesh, in_specs=placed, out_specs=P("freq", None), check_vma=False
    )
```

```python
import functools
import math

import jax
import jax.numpy as jnp
import numpy as np
from jax import lax
from jax.experimental import pallas as pl
from jax.experimental.pallas import tpu as pltpu
from jax.sharding import PartitionSpec as P

VS = 16
ITERS = 3
SCALE = 0.5
GROUP = 8
UNROLL = 8
LANES = 128
MESH = pl.DeviceIdType.MESH

precise = lax.Precision.HIGHEST
epsilon = 1e-06


def transform_tables(freq_total, samples):
    freq_index = np.arange(freq_total)[:, None] + 1
    time_index = np.arange(samples)[None, :]
    phases = (freq_index * time_index % samples) * (2.0 * math.pi / samples)
    factor = math.sqrt(2.0 / samples)
    return np.stack([factor * np.cos(phases), -factor * np.sin(phases)]).astype(np.float32)


def two_parts(field):
    high = field.astype(jnp.bfloat16)
    low = (field - high.astype(jnp.float32)).astype(jnp.bfloat16)
    return jnp.concatenate([high, low])


def product_of(rows, right, side):
    both = lax.dot_general(
        rows, right, (((1,), (side,)), ((), ())), preferred_element_type=jnp.float32
    )
    return both if rows.shape[0] == 2 * VS else both[: 2 * VS] + both[2 * VS :]


def iterate_weights(data_square, moments):
    model_norms = [jnp.sqrt(moments[2 * k]) for k in range(ITERS)]
    data_norms = [jnp.sqrt(data_square)] + [jnp.sqrt(moments[2 * k + 1]) for k in range(ITERS)]

    def ratio(top, bottom):
        return jnp.where(bottom > 0, top / jnp.where(bottom > 0, bottom, 1.0), 0.0)

    model_gram = [
        [ratio(ratio(moments[i + j], model_norms[i]), model_norms[j]) for j in range(ITERS)]
        for i in range(ITERS)
    ]

    def data_inner(i, j):
        low, high = min(i, j), max(i, j)
        if high == 0:
            return data_square
        if low == 0:
            return moments[high - 1]
        return moments[low + high - 1]

    data_gram = [
        [ratio(ratio(data_inner(i, j), data_norms[i]), data_norms[j]) for j in range(ITERS + 1)]
        for i in range(ITERS + 1)
    ]

    def norm_of(weights, gram):
        total = 0.0
        for i in range(len(weights)):
            total += weights[i] * weights[i] * ratio(gram[i][i], gram[i][i])
            for j in range(i):
                total += 2.0 * weights[i] * weights[j] * gram[i][j]
        return jnp.sqrt(jnp.maximum(total, 0.0) + epsilon)

    up = [ratio(data_norms[k + 1], model_norms[k]) / SCALE for k in range(ITERS)]
    down = [ratio(model_norms[k], data_norms[k]) / SCALE for k in range(ITERS)]
    zero = jnp.zeros_like(data_square)
    beta = jnp.sqrt(data_square + epsilon)
    data_vector = [data_norms[0] / beta] + [zero] * ITERS
    model_vector = [data_vector[k] * down[k] for k in range(ITERS)]
    alpha = norm_of(model_vector, model_gram)
    model_vector = [weight / alpha for weight in model_vector]
    direction = model_vector
    solution = [zero] * ITERS
    phi_bar = beta
    rho_bar = alpha
    for step in range(ITERS):
        image = [zero] + [model_vector[k] * up[k] for k in range(ITERS)]
        data_vector = [new - alpha * old for new, old in zip(image, data_vector)]
        beta = norm_of(data_vector, data_gram)
        data_vector = [weight / beta for weight in data_vector]
        rho_new = jnp.sqrt(rho_bar * rho_bar + beta * beta)
        cosine = rho_bar / rho_new
        sine_part = beta / rho_new
        phi_value = cosine * phi_bar
        phi_bar = sine_part * phi_bar
        solution = [
            old + phi_value / rho_new * weight for old, weight in zip(solution, direction)
        ]
        if step < ITERS - 1:
            image = [data_vector[k] * down[k] for k in range(ITERS)]
            model_vector = [new - beta * old for new, old in zip(image, model_vector)]
            alpha = norm_of(model_vector, model_gram)
            model_vector = [weight / alpha for weight in model_vector]
            theta = sine_part * alpha
            rho_bar = -cosine * alpha
            direction = [
                weight - theta / rho_new * old for weight, old in zip(model_vector, direction)
            ]
    return [ratio(weight, norm) for weight, norm in zip(solution, model_norms)]


def square_of(field):
    return jnp.broadcast_to(jnp.sum(field * field, keepdims=True), (1, 128))


def lsqr_kernel(
    panels,
    blocks,
    data_hbm,
    table_hbm,
    wave_hbm,
    spectrum_ref,
    data_ref,
    table_ref,
    wave_ref,
    lines_out,
    lines_in,
    data_rows,
    leaving,
    landed,
    parts,
    arrived,
    bases,
    parts_short,
    arrived_short,
    bases_short,
    sums_out,
    sums_in,
    across,
    load_sem,
    lines_send,
    lines_recv,
    trace_send,
    trace_recv,
    part_send,
    part_recv,
    base_send,
    base_recv,
    sums_send,
    sums_recv,
    across_send,
    across_recv,
):
    me = lax.axis_index("panel")
    freq = lax.axis_index("freq")
    panel_peers = [{"panel": (me + k) % panels} for k in range(1, panels)]

    loads = [
        pltpu.make_async_copy(data_hbm, data_ref, load_sem.at[0]),
        pltpu.make_async_copy(table_hbm, table_ref, load_sem.at[1]),
        pltpu.make_async_copy(wave_hbm.at[:, 0], wave_ref, load_sem.at[2]),
    ]
    for load in loads:
        load.start()

    barrier = pltpu.get_barrier_semaphore()
    for peer in panel_peers:
        pl.semaphore_signal(barrier, inc=1, device_id=peer, device_id_type=MESH)

    def for_others(body):
        groups = (blocks - 1) // UNROLL

        @pl.loop(0, groups)
        def _(group):
            for k in range(UNROLL):
                body(group * UNROLL + k + 1)

        for k in range(groups * UNROLL + 1, blocks):
            body(k)

    @for_others
    def _(k):
        peer = {"freq": lax.rem(freq + k, blocks)}
        pl.semaphore_signal(barrier, inc=1, device_id=peer, device_id_type=MESH)

    strips = blocks // VS
    chunk = bases.shape[-1] // strips
    half = leaving.shape[-1] // 2
    span = data_rows.shape[-1] // strips

    def slot_of(index):
        return lax.rem(index, strips) * VS + lax.div(index, strips)

    sent = []

    def copy_to(peer, source, target, send_sem, recv_sem):
        copy = pltpu.make_async_remote_copy(
            src_ref=source,
            dst_ref=target,
            send_sem=send_sem,
            recv_sem=recv_sem,
            device_id=peer,
            device_id_type=MESH,
        )
        copy.start()
        sent.append(copy)

    def arrival(ref, recv_sem):
        pltpu.make_async_copy(ref, ref, recv_sem).wait()

    def exchange(source, source_slot, target, target_slot, send_sem, recv_sem):
        target[target_slot(freq)] = source[source_slot(freq)]

        @for_others
        def _(k):
            peer = lax.rem(freq + k, blocks)
            pltpu.make_async_remote_copy(
                src_ref=source.at[source_slot(peer)],
                dst_ref=target.at[target_slot(freq)],
                send_sem=send_sem,
                recv_sem=recv_sem,
                device_id={"freq": peer},
                device_id_type=MESH,
            ).start()

    def exchanged(ref, sem):
        others = ref.at[pl.ds(0, blocks - 1)]
        pltpu.make_async_copy(others, others, sem).wait()

    def same(index):
        return index

    models = []

    def send_traces(step):
        model = models[step]
        for strip in range(strips):
            columns = slice(strip * chunk, (strip + 1) * chunk)
            slots = slice(strip * VS, (strip + 1) * VS)
            leaving[step, slots, 0, :chunk] = model[:VS, columns]
            leaving[step, slots, 0, half : half + chunk] = model[VS:, columns]
        exchange(
            leaving.at[step],
            slot_of,
            landed.at[step],
            same,
            trace_send.at[step],
            trace_recv.at[step],
        )

    lanes = lax.broadcasted_iota(jnp.int32, (1, LANES), 1)
    lines_out[...] = jnp.zeros_like(lines_out)
    loads[0].wait()
    loads[1].wait()
    data = data_ref[:, 0, :]
    squares = [square_of(data)]
    for part in range(2):
        first = part * (LANES // 2)
        lines_out[:, 0, first : first + data.shape[0]] = lax.dot_general(
            table_ref[part], data, (((1,), (1,)), ((), ())), precision=precise
        )
    pl.semaphore_wait(barrier, len(panel_peers) + blocks - 1)
    exchange(lines_out, same, lines_in, slot_of, lines_send, lines_recv)
    leaving[...] = jnp.zeros_like(leaving)
    loads[2].wait()
    exchanged(lines_in, lines_recv)
    for strip in range(strips):
        columns = slice(strip * span, (strip + 1) * span)
        slots = slice(strip * VS, (strip + 1) * VS)
        data_rows[:VS, columns] = lines_in[slots, 0, :span]
        data_rows[VS:, columns] = lines_in[slots, 0, LANES // 2 : LANES // 2 + span]
    rows = two_parts(data_rows[...])
    for step in range(ITERS):
        by_real = product_of(rows, wave_ref[0], 0)
        by_imag = product_of(rows, wave_ref[1], 0)
        real_part = SCALE * (by_real[:VS] + by_imag[VS:])
        imag_part = SCALE * (by_real[VS:] - by_imag[:VS])
        short = step != 1
        place = step // 2
        out_parts, in_parts, totals = (
            (parts_short, arrived_short, bases_short) if short else (parts, arrived, bases)
        )
        kind = out_parts.dtype
        out_parts[place, : panels // 2] = real_part.astype(kind).reshape(panels // 2, GROUP, -1)
        out_parts[place, panels // 2 :] = imag_part.astype(kind).reshape(panels // 2, GROUP, -1)
        for k in range(1, panels):
            copy_to(
                panel_peers[k - 1],
                out_parts.at[place, (me + k) % panels],
                in_parts.at[place, k - 1],
                part_send.at[step, k - 1],
                part_recv.at[step, k - 1],
            )
        if step > 0:
            send_traces(step - 1)
        total = out_parts[place, me].astype(jnp.float32)
        for k in range(1, panels):
            arrival(in_parts.at[place, k - 1], part_recv.at[step, k - 1])
            total = total + in_parts[place, k - 1].astype(jnp.float32)
        totals[place, me] = total.astype(kind)
        for k in range(1, panels):
            copy_to(
                panel_peers[k - 1],
                totals.at[place, me],
                totals.at[place, me],
                base_send.at[step, k - 1],
                base_recv.at[step, k - 1],
            )
        squares.append(square_of(totals[place, me].astype(jnp.float32)))
        for k in range(1, panels):
            arrival(totals.at[place, (me + panels - k) % panels], base_recv.at[step, k - 1])
        model = totals[place].astype(jnp.float32).reshape(2 * VS, -1)
        models.append(model)
        model_rows = model.astype(jnp.bfloat16) if short else two_parts(model)
        by_real = product_of(model_rows, wave_ref[0], 1)
        by_imag = product_of(model_rows, wave_ref[1], 1)
        image = SCALE * jnp.concatenate(
            [by_real[:VS] - by_imag[VS:], by_imag[:VS] + by_real[VS:]]
        )
        squares.append(square_of(image))
        if step < ITERS - 1:
            rows = two_parts(image)

    sums_out[0] = sum(
        jnp.where(lanes == k, square, 0.0) for k, square in enumerate(squares)
    )
    exchange(sums_out, lambda index: 0, sums_in, same, sums_send, sums_recv)
    send_traces(ITERS - 1)
    exchanged(sums_in, sums_recv)
    across[me] = jnp.sum(sums_in[...], axis=0)
    for k in range(1, panels):
        copy_to(
            panel_peers[k - 1],
            across.at[me],
            across.at[me],
            across_send.at[k - 1],
            across_recv.at[k - 1],
        )
    for k in range(1, panels):
        arrival(across.at[(me + panels - k) % panels], across_recv.at[k - 1])
    total = across[0]
    for k in range(1, panels):
        total = total + across[k]
    squares = [
        jnp.broadcast_to(jnp.sum(jnp.where(lanes == k, total, 0.0), keepdims=True), (1, LANES))
        for k in range(len(squares))
    ]
    weights = iterate_weights(squares[0], squares[1:])
    weights = [jnp.concatenate([weight] * (2 * half // LANES), axis=1) for weight in weights]
    for step in range(ITERS):
        exchanged(landed.at[step], trace_recv.at[step])
    for first in range(0, blocks, VS):
        rows = slice(first, first + VS)
        spectrum_ref[rows] = sum(
            weight[None] * landed[step, rows] for step, weight in enumerate(weights)
        )
    for copy in sent:
        copy.wait_send()
    exchanged(lines_in, lines_send)
    exchanged(sums_in, sums_send)
    for step in range(ITERS):
        exchanged(landed.at[step], trace_send.at[step])


def solved_spectra(data, table, wave, panels, blocks):
    sources = wave.shape[3]
    quarter = (GROUP, sources)
    row = (1, LANES)
    half = -(-2 * VS * sources // (2 * blocks) // LANES) * LANES
    dma = pltpu.SemaphoreType.DMA
    return pl.pallas_call(
        functools.partial(lsqr_kernel, panels, blocks),
        out_shape=jax.ShapeDtypeStruct((blocks, 1, 2 * half), jnp.float32),
        in_specs=[pl.BlockSpec(memory_space=pl.ANY)] * 3,
        out_specs=pl.BlockSpec(memory_space=pltpu.VMEM),
        scratch_shapes=[
            pltpu.VMEM(data.shape, jnp.float32),
            pltpu.VMEM(table.shape, jnp.float32),
            pltpu.VMEM((2, *wave.shape[2:]), jnp.bfloat16),
            pltpu.VMEM((blocks, *row), jnp.float32),
            pltpu.VMEM((blocks, *row), jnp.float32),
            pltpu.VMEM((2 * VS, wave.shape[2]), jnp.float32),
            pltpu.VMEM((ITERS, blocks, 1, 2 * half), jnp.float32),
            pltpu.VMEM((ITERS, blocks, 1, 2 * half), jnp.float32),
            pltpu.VMEM((1, panels, *quarter), jnp.float32),
            pltpu.VMEM((1, panels - 1, *quarter), jnp.float32),
            pltpu.VMEM((1, panels, *quarter), jnp.float32),
            pltpu.VMEM((2, panels, *quarter), jnp.bfloat16),
            pltpu.VMEM((2, panels - 1, *quarter), jnp.bfloat16),
            pltpu.VMEM((2, panels, *quarter), jnp.bfloat16),
            pltpu.VMEM((1, *row), jnp.float32),
            pltpu.VMEM((blocks, *row), jnp.float32),
            pltpu.VMEM((panels, *row), jnp.float32),
            dma((3,)),
            dma,
            dma,
            dma((ITERS,)),
            dma((ITERS,)),
            dma((ITERS, panels - 1)),
            dma((ITERS, panels - 1)),
            dma((ITERS, panels - 1)),
            dma((ITERS, panels - 1)),
            dma,
            dma,
            dma((panels - 1,)),
            dma((panels - 1,)),
        ],
        compiler_params=pltpu.CompilerParams(
            collective_id=0, has_side_effects=True, vmem_limit_bytes=63 * 1024 * 1024
        ),
    )(data, table, wave)


def on_device(wave, observed):
    blocks = lax.axis_size("freq")
    panels = lax.axis_size("panel")
    table = jnp.asarray(transform_tables(blocks, observed.shape[2]))
    traces = observed.transpose(1, 0, 2)
    spectra = solved_spectra(traces, table, wave, panels, blocks)
    spectra = spectra.reshape(blocks, 2, -1)[:, :, : VS * wave.shape[3] // blocks]
    return jnp.einsum("jcr,cjt->rt", spectra, table, precision=precise)


def solution(mesh):
    placed = (P(None, "freq", "panel", None), P("panel", "freq", None))
    return jax.shard_map(
        on_device, mesh=mesh, in_specs=placed, out_specs=P("freq", None), check_vma=False
    )
```

```python
import functools
import math

import jax
import jax.numpy as jnp
import numpy as np
from jax import lax
from jax.experimental import pallas as pl
from jax.experimental.pallas import tpu as pltpu
from jax.sharding import PartitionSpec as P

VS = 16
ITERS = 3
SCALE = 0.5
GROUP = 8
UNROLL = 7
LANES = 128
MESH = pl.DeviceIdType.MESH

precise = lax.Precision.HIGHEST
epsilon = 1e-06


def transform_tables(freq_total, samples):
    freq_index = np.arange(freq_total)[:, None] + 1
    time_index = np.arange(samples)[None, :]
    phases = (freq_index * time_index % samples) * (2.0 * math.pi / samples)
    factor = math.sqrt(2.0 / samples)
    return np.stack([factor * np.cos(phases), -factor * np.sin(phases)]).astype(np.float32)


def two_parts(field):
    high = field.astype(jnp.bfloat16)
    low = (field - high.astype(jnp.float32)).astype(jnp.bfloat16)
    return jnp.concatenate([high, low])


def product_of(rows, right, side):
    both = lax.dot_general(
        rows, right, (((1,), (side,)), ((), ())), preferred_element_type=jnp.float32
    )
    return both if rows.shape[0] == 2 * VS else both[: 2 * VS] + both[2 * VS :]


def iterate_weights(data_square, moments):
    model_norms = [jnp.sqrt(moments[2 * k]) for k in range(ITERS)]
    data_norms = [jnp.sqrt(data_square)] + [jnp.sqrt(moments[2 * k + 1]) for k in range(ITERS)]

    def ratio(top, bottom):
        return jnp.where(bottom > 0, top / jnp.where(bottom > 0, bottom, 1.0), 0.0)

    model_gram = [
        [ratio(ratio(moments[i + j], model_norms[i]), model_norms[j]) for j in range(ITERS)]
        for i in range(ITERS)
    ]

    def data_inner(i, j):
        low, high = min(i, j), max(i, j)
        if high == 0:
            return data_square
        if low == 0:
            return moments[high - 1]
        return moments[low + high - 1]

    data_gram = [
        [ratio(ratio(data_inner(i, j), data_norms[i]), data_norms[j]) for j in range(ITERS + 1)]
        for i in range(ITERS + 1)
    ]

    def norm_of(weights, gram):
        total = 0.0
        for i in range(len(weights)):
            total += weights[i] * weights[i] * ratio(gram[i][i], gram[i][i])
            for j in range(i):
                total += 2.0 * weights[i] * weights[j] * gram[i][j]
        return jnp.sqrt(jnp.maximum(total, 0.0) + epsilon)

    up = [ratio(data_norms[k + 1], model_norms[k]) / SCALE for k in range(ITERS)]
    down = [ratio(model_norms[k], data_norms[k]) / SCALE for k in range(ITERS)]
    zero = jnp.zeros_like(data_square)
    beta = jnp.sqrt(data_square + epsilon)
    data_vector = [data_norms[0] / beta] + [zero] * ITERS
    model_vector = [data_vector[k] * down[k] for k in range(ITERS)]
    alpha = norm_of(model_vector, model_gram)
    model_vector = [weight / alpha for weight in model_vector]
    direction = model_vector
    solution = [zero] * ITERS
    phi_bar = beta
    rho_bar = alpha
    for step in range(ITERS):
        image = [zero] + [model_vector[k] * up[k] for k in range(ITERS)]
        data_vector = [new - alpha * old for new, old in zip(image, data_vector)]
        beta = norm_of(data_vector, data_gram)
        data_vector = [weight / beta for weight in data_vector]
        rho_new = jnp.sqrt(rho_bar * rho_bar + beta * beta)
        cosine = rho_bar / rho_new
        sine_part = beta / rho_new
        phi_value = cosine * phi_bar
        phi_bar = sine_part * phi_bar
        solution = [
            old + phi_value / rho_new * weight for old, weight in zip(solution, direction)
        ]
        if step < ITERS - 1:
            image = [data_vector[k] * down[k] for k in range(ITERS)]
            model_vector = [new - beta * old for new, old in zip(image, model_vector)]
            alpha = norm_of(model_vector, model_gram)
            model_vector = [weight / alpha for weight in model_vector]
            theta = sine_part * alpha
            rho_bar = -cosine * alpha
            direction = [
                weight - theta / rho_new * old for weight, old in zip(model_vector, direction)
            ]
    return [ratio(weight, norm) for weight, norm in zip(solution, model_norms)]


def square_of(field):
    return jnp.broadcast_to(jnp.sum(field * field, keepdims=True), (1, 128))


def lsqr_kernel(
    panels,
    blocks,
    data_hbm,
    table_hbm,
    wave_hbm,
    spectrum_ref,
    data_ref,
    table_ref,
    wave_ref,
    lines_out,
    lines_in,
    data_rows,
    leaving,
    landed,
    parts,
    arrived,
    bases,
    parts_short,
    arrived_short,
    bases_short,
    sums_out,
    sums_in,
    across,
    load_sem,
    lines_send,
    lines_recv,
    trace_send,
    trace_recv,
    part_send,
    part_recv,
    base_send,
    base_recv,
    sums_send,
    sums_recv,
    across_send,
    across_recv,
):
    me = lax.axis_index("panel")
    freq = lax.axis_index("freq")
    farthest = sorted(range(1, panels), key=lambda k: -min(k, panels - k))
    panel_peers = [{"panel": (me + k) % panels} for k in range(1, panels)]

    loads = [
        pltpu.make_async_copy(data_hbm, data_ref, load_sem.at[0]),
        pltpu.make_async_copy(table_hbm, table_ref, load_sem.at[1]),
        pltpu.make_async_copy(wave_hbm.at[:, 0], wave_ref, load_sem.at[2]),
    ]
    for load in loads:
        load.start()

    barrier = pltpu.get_barrier_semaphore()
    for peer in panel_peers:
        pl.semaphore_signal(barrier, inc=1, device_id=peer, device_id_type=MESH)

    def for_others(body):
        middle = blocks // 2
        groups = (middle - 1) // UNROLL

        def pair(step):
            body(middle + step)
            body(middle - step)

        body(middle)

        @pl.loop(0, groups)
        def _(group):
            for k in range(UNROLL):
                pair(group * UNROLL + k + 1)

        for k in range(groups * UNROLL + 1, middle):
            pair(k)

    @for_others
    def _(k):
        peer = {"freq": lax.rem(freq + k, blocks)}
        pl.semaphore_signal(barrier, inc=1, device_id=peer, device_id_type=MESH)

    strips = blocks // VS
    chunk = bases.shape[-1] // strips
    half = leaving.shape[-1] // 2
    span = data_rows.shape[-1] // strips

    def slot_of(index):
        return lax.rem(index, strips) * VS + lax.div(index, strips)

    sent = []

    def copy_to(peer, source, target, send_sem, recv_sem):
        copy = pltpu.make_async_remote_copy(
            src_ref=source,
            dst_ref=target,
            send_sem=send_sem,
            recv_sem=recv_sem,
            device_id=peer,
            device_id_type=MESH,
        )
        copy.start()
        sent.append(copy)

    def arrival(ref, recv_sem):
        pltpu.make_async_copy(ref, ref, recv_sem).wait()

    def exchange(source, source_slot, target, target_slot, send_sem, recv_sem):
        target[target_slot(freq)] = source[source_slot(freq)]

        @for_others
        def _(k):
            peer = lax.rem(freq + k, blocks)
            pltpu.make_async_remote_copy(
                src_ref=source.at[source_slot(peer)],
                dst_ref=target.at[target_slot(freq)],
                send_sem=send_sem,
                recv_sem=recv_sem,
                device_id={"freq": peer},
                device_id_type=MESH,
            ).start()

    def exchanged(ref, sem):
        others = ref.at[pl.ds(0, blocks - 1)]
        pltpu.make_async_copy(others, others, sem).wait()

    def same(index):
        return index

    models = []

    def send_traces(step):
        model = models[step]
        for strip in range(strips):
            columns = slice(strip * chunk, (strip + 1) * chunk)
            slots = slice(strip * VS, (strip + 1) * VS)
            leaving[step, slots, 0, :chunk] = model[:VS, columns]
            leaving[step, slots, 0, half : half + chunk] = model[VS:, columns]
        exchange(
            leaving.at[step],
            slot_of,
            landed.at[step],
            same,
            trace_send.at[step],
            trace_recv.at[step],
        )

    lanes = lax.broadcasted_iota(jnp.int32, (1, LANES), 1)
    lines_out[...] = jnp.zeros_like(lines_out)
    loads[0].wait()
    loads[1].wait()
    data = data_ref[:, 0, :]
    squares = [square_of(data)]
    for part in range(2):
        first = part * (LANES // 2)
        lines_out[:, 0, first : first + data.shape[0]] = lax.dot_general(
            table_ref[part], data, (((1,), (1,)), ((), ())), precision=precise
        )
    pl.semaphore_wait(barrier, len(panel_peers) + blocks - 1)
    exchange(lines_out, same, lines_in, slot_of, lines_send, lines_recv)
    leaving[...] = jnp.zeros_like(leaving)
    loads[2].wait()
    exchanged(lines_in, lines_recv)
    for strip in range(strips):
        columns = slice(strip * span, (strip + 1) * span)
        slots = slice(strip * VS, (strip + 1) * VS)
        data_rows[:VS, columns] = lines_in[slots, 0, :span]
        data_rows[VS:, columns] = lines_in[slots, 0, LANES // 2 : LANES // 2 + span]
    rows = two_parts(data_rows[...])
    for step in range(ITERS):
        by_real = product_of(rows, wave_ref[0], 0)
        by_imag = product_of(rows, wave_ref[1], 0)
        real_part = SCALE * (by_real[:VS] + by_imag[VS:])
        imag_part = SCALE * (by_real[VS:] - by_imag[:VS])
        short = step == 0
        place = 0 if short else step - 1
        out_parts, in_parts, totals = (
            (parts_short, arrived_short, bases_short) if short else (parts, arrived, bases)
        )
        kind = out_parts.dtype
        out_parts[place, : panels // 2] = real_part.astype(kind).reshape(panels // 2, GROUP, -1)
        out_parts[place, panels // 2 :] = imag_part.astype(kind).reshape(panels // 2, GROUP, -1)
        for k in farthest:
            copy_to(
                panel_peers[k - 1],
                out_parts.at[place, (me + k) % panels],
                in_parts.at[place, k - 1],
                part_send.at[step, k - 1],
                part_recv.at[step, k - 1],
            )
        if step > 0:
            send_traces(step - 1)
        total = out_parts[place, me].astype(jnp.float32)
        for k in range(1, panels):
            arrival(in_parts.at[place, k - 1], part_recv.at[step, k - 1])
            total = total + in_parts[place, k - 1].astype(jnp.float32)
        totals[place, me] = total.astype(kind)
        for k in farthest:
            copy_to(
                panel_peers[k - 1],
                totals.at[place, me],
                totals.at[place, me],
                base_send.at[step, k - 1],
                base_recv.at[step, k - 1],
            )
        squares.append(square_of(totals[place, me].astype(jnp.float32)))
        for k in range(1, panels):
            arrival(totals.at[place, (me + panels - k) % panels], base_recv.at[step, k - 1])
        model = totals[place].astype(jnp.float32).reshape(2 * VS, -1)
        models.append(model)
        model_rows = model.astype(jnp.bfloat16) if short else two_parts(model)
        by_real = product_of(model_rows, wave_ref[0], 1)
        by_imag = product_of(model_rows, wave_ref[1], 1)
        image = SCALE * jnp.concatenate(
            [by_real[:VS] - by_imag[VS:], by_imag[:VS] + by_real[VS:]]
        )
        squares.append(square_of(image))
        if step < ITERS - 1:
            rows = two_parts(image)

    sums_out[0] = sum(
        jnp.where(lanes == k, square, 0.0) for k, square in enumerate(squares)
    )
    exchange(sums_out, lambda index: 0, sums_in, same, sums_send, sums_recv)
    send_traces(ITERS - 1)
    exchanged(sums_in, sums_recv)
    across[me] = jnp.sum(sums_in[...], axis=0)
    for k in farthest:
        copy_to(
            panel_peers[k - 1],
            across.at[me],
            across.at[me],
            across_send.at[k - 1],
            across_recv.at[k - 1],
        )
    for k in range(1, panels):
        arrival(across.at[(me + panels - k) % panels], across_recv.at[k - 1])
    total = across[0]
    for k in range(1, panels):
        total = total + across[k]
    squares = [
        jnp.broadcast_to(jnp.sum(jnp.where(lanes == k, total, 0.0), keepdims=True), (1, LANES))
        for k in range(len(squares))
    ]
    weights = iterate_weights(squares[0], squares[1:])
    weights = [jnp.concatenate([weight] * (2 * half // LANES), axis=1) for weight in weights]
    for step in range(ITERS):
        exchanged(landed.at[step], trace_recv.at[step])
    for first in range(0, blocks, VS):
        rows = slice(first, first + VS)
        spectrum_ref[rows] = sum(
            weight[None] * landed[step, rows] for step, weight in enumerate(weights)
        )
    for copy in sent:
        copy.wait_send()
    exchanged(lines_in, lines_send)
    exchanged(sums_in, sums_send)
    for step in range(ITERS):
        exchanged(landed.at[step], trace_send.at[step])


def solved_spectra(data, table, wave, panels, blocks):
    sources = wave.shape[3]
    quarter = (GROUP, sources)
    row = (1, LANES)
    half = -(-2 * VS * sources // (2 * blocks) // LANES) * LANES
    dma = pltpu.SemaphoreType.DMA
    return pl.pallas_call(
        functools.partial(lsqr_kernel, panels, blocks),
        out_shape=jax.ShapeDtypeStruct((blocks, 1, 2 * half), jnp.float32),
        in_specs=[pl.BlockSpec(memory_space=pl.ANY)] * 3,
        out_specs=pl.BlockSpec(memory_space=pltpu.VMEM),
        scratch_shapes=[
            pltpu.VMEM(data.shape, jnp.float32),
            pltpu.VMEM(table.shape, jnp.float32),
            pltpu.VMEM((2, *wave.shape[2:]), jnp.bfloat16),
            pltpu.VMEM((blocks, *row), jnp.float32),
            pltpu.VMEM((blocks, *row), jnp.float32),
            pltpu.VMEM((2 * VS, wave.shape[2]), jnp.float32),
            pltpu.VMEM((ITERS, blocks, 1, 2 * half), jnp.float32),
            pltpu.VMEM((ITERS, blocks, 1, 2 * half), jnp.float32),
            pltpu.VMEM((ITERS - 1, panels, *quarter), jnp.float32),
            pltpu.VMEM((ITERS - 1, panels - 1, *quarter), jnp.float32),
            pltpu.VMEM((ITERS - 1, panels, *quarter), jnp.float32),
            pltpu.VMEM((1, panels, *quarter), jnp.bfloat16),
            pltpu.VMEM((1, panels - 1, *quarter), jnp.bfloat16),
            pltpu.VMEM((1, panels, *quarter), jnp.bfloat16),
            pltpu.VMEM((1, *row), jnp.float32),
            pltpu.VMEM((blocks, *row), jnp.float32),
            pltpu.VMEM((panels, *row), jnp.float32),
            dma((3,)),
            dma,
            dma,
            dma((ITERS,)),
            dma((ITERS,)),
            dma((ITERS, panels - 1)),
            dma((ITERS, panels - 1)),
            dma((ITERS, panels - 1)),
            dma((ITERS, panels - 1)),
            dma,
            dma,
            dma((panels - 1,)),
            dma((panels - 1,)),
        ],
        compiler_params=pltpu.CompilerParams(
            collective_id=0, has_side_effects=True, vmem_limit_bytes=63 * 1024 * 1024
        ),
    )(data, table, wave)


def on_device(wave, observed):
    blocks = lax.axis_size("freq")
    panels = lax.axis_size("panel")
    table = jnp.asarray(transform_tables(blocks, observed.shape[2]))
    traces = observed.transpose(1, 0, 2)
    spectra = solved_spectra(traces, table, wave, panels, blocks)
    spectra = spectra.reshape(blocks, 2, -1)[:, :, : VS * wave.shape[3] // blocks]
    return jnp.einsum("jcr,cjt->rt", spectra, table, precision=precise)


def solution(mesh):
    placed = (P(None, "freq", "panel", None), P("panel", "freq", None))
    return jax.shard_map(
        on_device, mesh=mesh, in_specs=placed, out_specs=P("freq", None), check_vma=False
    )
```
